256 devices in a mesh: ifg: 64 (over x, z, core), grp: 4 (over y).
Axes of the slice: x: 4, y: 4, z: 8, core: 2. Of those that a mesh axis runs over, the one named last changes fastest.
Arguments:
- phases: bfloat16 [1024, 4, 262144], P('ifg', 'grp'), may hold values from -6 to 6
- date_pairs: int32 [2, 1024], replicated, may hold values from 0 to 199, as said below
- pair_counts: int32 [16], replicated, may hold values from 128 to 1024, as said below
- group_ids: int32 [4, 1024], P(None, 'ifg'), may hold values from 0 to 15, as said below
Outputs:
- series: float32 [4, 200, 262144], P('grp', None, 'ifg')
The draws below stay inside these ranges and needn't reach their ends.
Inputs may be any that keep to these rules, and one draw needn't show every extreme that they name: date_pairs[0, k] < date_pairs[1, k]; the baseline date_pairs[1, k] - date_pairs[0, k] lies in 1 to 25 and never falls as k grows. `pair_counts`: each count is 128 times a power of two; some class has all 1024 interferograms and some has 128. `group_ids`: constant over each aligned run of 8 blocks of a sub-strip.
All inputs are finite; a program needn't handle non-finite values.
Results may differ from the reference program's by a relative error of at most 0.0003.
Values may be sent and summed in bfloat16 or wider, within the bound.
A program may use at most 128 MiB of HBM per device.

```python
import jax
import jax.numpy as jnp
from jax import lax

K = 1024
M = 200
NG = 16
BLOCK = 256
RUN = 8
SLAB = 128
STRIPS = 4
SBLK = 1024
SPIX = 262144


def draw_date_pairs(key, part):
    first_key, second_key = jax.random.split(jax.random.fold_in(key, 11))
    baseline = jnp.sort(jax.random.randint(first_key, (K,), 1, M // 8 + 1))
    earlier = jax.random.randint(second_key, (K,), 0, M - baseline)
    return jnp.stack([earlier, earlier + baseline]).astype(jnp.int32)


def draw_pair_counts(key, part):
    levels = jax.random.randint(jax.random.fold_in(key, 23), (NG,), 0, 4)
    counts = K // 8 * jnp.left_shift(jnp.ones((NG,), jnp.int32), levels)
    counts = counts.at[0].set(K).at[1].set(K // 8)
    return counts.astype(jnp.int32)


def draw_group_ids(key, part):
    run_groups = jax.random.randint(jax.random.fold_in(key, 37), (STRIPS, SBLK // RUN), 0, NG)
    return jnp.repeat(run_groups, RUN, axis=1).astype(jnp.int32)


def shard_levels(key, dims, cuts, smallest, top_value):
    loudness = 1.0
    for axis_at, blocks in cuts:
        draws = jax.random.uniform(jax.random.fold_in(jax.random.fold_in(key, 6), axis_at), (blocks,), jnp.float32, smallest / len(cuts), top_value / len(cuts))
        loudness = loudness * jnp.repeat(jnp.exp(draws), dims[axis_at] // blocks).reshape((-1,) + (1,) * (len(dims) - 1 - axis_at))
    return loudness


def noise(stream_key, extent, width, bound, cuts=(), held_as=jnp.bfloat16):
    factor_of = shard_levels(stream_key, extent, cuts, -0.22, 0.18) if cuts else 1.0
    values = jax.random.normal(stream_key, extent, jnp.float32) * width * factor_of
    return jnp.minimum(jnp.maximum(values, -bound), bound).astype(held_as)


def setup_inputs(seed: int = 0) -> dict:
    arg_keys = jax.random.split(jax.random.key(seed), 5)
    phases = noise(arg_keys[0], (K, STRIPS, SPIX), 1.0, 6.0, ((0, 64), (1, 4)))
    date_pairs = draw_date_pairs(jax.random.fold_in(arg_keys[4], 71), 0)
    pair_counts = draw_pair_counts(jax.random.fold_in(arg_keys[4], 71), 0)
    group_ids = draw_group_ids(jax.random.fold_in(arg_keys[4], 71), 0)
    return {"phases": phases, "date_pairs": date_pairs, "pair_counts": pair_counts, "group_ids": group_ids}


damping = 1.0

def reference(phases, date_pairs, pair_counts, group_ids):
    date_index = jnp.arange(M, dtype=jnp.int32)
    design = (date_index[None, :] == date_pairs[1][:, None]).astype(jnp.float32) - (date_index[None, :] == date_pairs[0][:, None]).astype(jnp.float32)
    row_index = jnp.arange(K, dtype=jnp.int32)
    keep_mask = (row_index[None, :] < pair_counts[:, None]).astype(jnp.float32)
    identity = jnp.eye(M, dtype=jnp.float32)

    def class_gram(mask_row):
        return jnp.dot((design * mask_row[:, None]).T, design, precision=lax.Precision.HIGHEST) + damping * identity
    gram_sums = lax.map(class_gram, keep_mask)
    factors = jnp.linalg.cholesky(gram_sums)

    def strip_solve(strip_index):
        strip_data = lax.dynamic_index_in_dim(phases, strip_index, 1, keepdims=False)
        block_groups = lax.dynamic_index_in_dim(group_ids, strip_index, 0, keepdims=False)
        slab_count = pair_counts[block_groups] // SLAB

        def add_slab(slab_index, running):
            data_slab = lax.dynamic_slice_in_dim(strip_data, slab_index * SLAB, SLAB, 0).astype(jnp.float32)
            design_slab = lax.dynamic_slice_in_dim(design, slab_index * SLAB, SLAB, 0)
            slab_term = jnp.dot(design_slab.T, data_slab, precision=lax.Precision.HIGHEST)
            weight = jnp.repeat((slab_index < slab_count).astype(jnp.float32), BLOCK)
            return running + slab_term * weight[None, :]
        right_side = lax.fori_loop(0, K // SLAB, add_slab, jnp.zeros((M, SPIX), jnp.float32))
        per_block = right_side.reshape(M, SBLK, BLOCK).transpose(1, 0, 2)

        def solve_block(pieces):
            block_rhs, group = pieces
            return jax.scipy.linalg.cho_solve((factors[group], True), block_rhs)
        solved = lax.map(solve_block, (per_block, block_groups))
        return solved.transpose(1, 0, 2).reshape(M, SPIX)
    return lax.map(strip_solve, jnp.arange(STRIPS, dtype=jnp.int32))
```

```python
import jax
import jax.numpy as jnp
from jax import lax
from jax.experimental import pallas as pl
from jax.experimental.pallas import tpu as pltpu
from jax.sharding import PartitionSpec as P

M = 200
MP = 208
PIX = 4096
HALF = 2048
CPX = 512
NC = PIX // CPX
LOOK = 4
LAG = 1
MESH = pl.DeviceIdType.MESH
OWN_BLOCK = (0, 0, 0)
LEFT = ((0, -1, 128), (-1, -2, 256), (-2, -3, 384))
RIGHT = ((0, 1, 640), (1, 2, 768), (2, 3, 896))
FAR = ((-3, -4, 512), (3, 4, 512))


def split3(value):
    high = value.astype(jnp.bfloat16)
    rest = value - high.astype(jnp.float32)
    middle = rest.astype(jnp.bfloat16)
    low = (rest - middle.astype(jnp.float32)).astype(jnp.bfloat16)
    return high, middle, low


def body(
    src, dates, hot, out,
    land, inverse, design, near_hot, w_own, w_left, w_right, sums_out, sums_in, scale_out, scale_in,
    raw_send, raw_recv, hot_send, hot_recv, sum_send, sum_recv, scale_send, scale_recv,
):
    me = lax.axis_index("ifg")
    core = lax.rem(me, 2)
    z = lax.rem(lax.div(me, 2), 8)
    x = lax.div(me, 16)

    def device(x_at, z_at, core_at):
        return lax.rem(x_at, 4) * 16 + lax.rem(z_at + 16, 8) * 2 + lax.rem(core_at, 2)

    left, right = device(x, z - 1, core), device(x, z + 1, core)

    barrier = pltpu.get_barrier_semaphore()

    def greet(step, carry):
        peer = device(x + lax.div(step, 2), z, core + lax.rem(step, 2))
        for offset in (-3, -2, -1, 1, 2, 3):
            there = device(x + lax.div(step, 2), z + offset, core + lax.rem(step, 2))
            pl.semaphore_signal(barrier, inc=1, device_id={"ifg": there}, device_id_type=MESH)

        @pl.when(step > 0)
        def _():
            pl.semaphore_signal(barrier, inc=1, device_id={"ifg": peer}, device_id_type=MESH)

        return carry

    lax.fori_loop(0, 8, greet, 0)
    pl.semaphore_wait(barrier, 55)

    hot_copies = []
    for side, there in ((0, right), (1, left)):
        copy = pltpu.make_async_remote_copy(
            src_ref=hot, dst_ref=near_hot.at[side], send_sem=hot_send.at[side], recv_sem=hot_recv.at[side],
            device_id={"ifg": there}, device_id_type=MESH,
        )
        copy.start()
        hot_copies.append(copy)

    my_rows = x * 32 + core * 16

    def raw_parts(block, chunk, x_at, core_at):
        helper, owner, first = block
        there = device(x_at, z + helper, core_at)
        owner_index = device(x_at, z + owner, core_at)
        columns = pl.ds(pl.multiple_of(owner_index * PIX + chunk * CPX, 128), CPX)
        rows = pl.ds(pl.multiple_of(first + my_rows, 16), 16)
        landing = pl.ds(pl.multiple_of(chunk * CPX, 128), CPX)
        return src.at[:, columns], land.at[rows, landing], there

    def raw_blocks(half):
        near = [OWN_BLOCK, LEFT[0], RIGHT[0]]
        far = [FAR[half], LEFT[2], RIGHT[2], LEFT[1], RIGHT[1]]
        return near, far

    def send_raw(chunk, half):
        near, far = raw_blocks(half)

        def remote(block, x_at, core_at):
            source, target, there = raw_parts(block, chunk, x_at, core_at)
            pltpu.make_async_remote_copy(
                src_ref=source, dst_ref=target, send_sem=raw_send.at[chunk], recv_sem=raw_recv.at[chunk],
                device_id={"ifg": there}, device_id_type=MESH,
            ).start()

        for block in far:
            remote(block, x, core)

        def peer(step, carry):
            for block in far + near:
                remote(block, x + lax.div(step, 2), core + lax.rem(step, 2))
            return carry

        lax.fori_loop(1, 8, peer, 0)
        for block in near:
            source, target, _ = raw_parts(block, chunk, x, core)
            pltpu.make_async_copy(source, target, raw_recv.at[chunk]).start()

    def wait_raw(chunk, sem, rows):
        view = land.at[pl.ds(0, rows), pl.ds(pl.multiple_of(chunk * CPX, 128), CPX)]
        pltpu.make_async_copy(view, view, sem.at[chunk]).wait()

    for chunk in range(LOOK):
        send_raw(chunk, chunk // (NC // 2))

    date_at = lax.broadcasted_iota(jnp.int32, (256, 1024), 0)
    signs = (date_at == dates[1:2, :]).astype(jnp.float32) - (date_at == dates[0:1, :]).astype(jnp.float32)
    design[...] = signs.astype(jnp.bfloat16)
    place = lax.broadcasted_iota(jnp.int32, (1, 1024), 1)
    pair = ((place >> 5) & 3) * 256 + (place >> 7) * 32 + (place & 31)
    eye = (
        lax.broadcasted_iota(jnp.int32, (MP, 256), 0) == lax.broadcasted_iota(jnp.int32, (MP, 256), 1)
    ).astype(jnp.float32)
    keep = [(pair < (128 << level)).astype(jnp.float32) for level in range(4)]
    for level in range(4):
        gram = lax.dot_general(
            design[0:MP, :], (signs * keep[level]).astype(jnp.bfloat16), (((1,), (1,)), ((), ())),
            preferred_element_type=jnp.float32,
        )
        inverse[level] = gram + eye
    lane = lax.broadcasted_iota(jnp.int32, (1, 1, 256), 2)
    lane_half = lax.broadcasted_iota(jnp.int32, (1, 1, 128), 2)

    def eliminate(side):
        mine, other = slice(side * 128, side * 128 + 128), slice(128 - side * 128, 256 - side * 128)

        def step(index, carry):
            hit = lane_half == index - side * 128
            row = inverse[:, pl.ds(index, 1), :]
            block = inverse[:, :, mine]
            column = jnp.sum(jnp.where(hit, block, 0.0), axis=2, keepdims=True)
            pivot = 1.0 / jnp.sum(jnp.where(hit, row[:, :, mine], 0.0), axis=2, keepdims=True)
            scaled = jnp.where(lane == index, pivot, row * pivot)
            inverse[:, :, mine] = jnp.where(hit, 0.0, block) - column * scaled[:, :, mine]
            inverse[:, :, other] = inverse[:, :, other] - column * scaled[:, :, other]
            inverse[:, pl.ds(index, 1), :] = scaled
            return carry

        return step

    lax.fori_loop(0, 128, eliminate(0), 0)
    lax.fori_loop(128, M, eliminate(1), 0)

    for copy in hot_copies:
        copy.wait()

    def weights(flags, run, blocks, target):
        flag = [flags[2 * level + run : 2 * level + run + 1, 0:1] for level in range(4)]
        parts = split3(sum(flag[level] * inverse[level] for level in range(4)))
        column = lax.broadcasted_iota(jnp.int32, (1, 128), 1)
        for at, offset in enumerate(blocks):
            z_at = lax.rem(z + offset + 16, 8)
            block = design[:, pl.ds(pl.multiple_of(z_at * 128, 128), 128)]
            value = sum(jnp.dot(part, block, preferred_element_type=jnp.float32) for part in parts)
            pair_at = (column >> 5) * 256 + z_at * 32 + (column & 31)
            value = value * sum(flag[level] * (pair_at < (128 << level)).astype(jnp.float32) for level in range(4))
            high = value.astype(jnp.bfloat16)
            low = (value - high.astype(jnp.float32)).astype(jnp.bfloat16)
            target[run, 0:MP, at * 128 : at * 128 + 128] = high
            target[run, MP : 2 * MP, at * 128 : at * 128 + 128] = low

    for run in range(2):
        weights(hot, run, (0,), w_own)
        weights(near_hot.at[0], run, (0, 1, 2, 3)[: 4 - run], w_left)
        weights(near_hot.at[1], run, (0, -1, -2) if run == 0 else (-3, 0, -1, -2), w_right)

    def apply(weight, chunk, first, depth):
        data = land[first : first + depth, pl.ds(pl.multiple_of(chunk * CPX, 128), CPX)]
        both = jnp.dot(weight, data, preferred_element_type=jnp.float32)
        return both[0:MP] + both[MP : 2 * MP]

    def sum_copies(chunk):
        copies = []
        for side, there in ((0, left), (1, right)):
            copies.append(pltpu.make_async_remote_copy(
                src_ref=sums_out.at[side, chunk], dst_ref=sums_in.at[side, chunk],
                send_sem=sum_send.at[side, chunk], recv_sem=sum_recv.at[side, chunk],
                device_id={"ifg": there}, device_id_type=MESH,
            ))
            copies.append(pltpu.make_async_remote_copy(
                src_ref=scale_out.at[side, chunk], dst_ref=scale_in.at[side, chunk],
                send_sem=scale_send.at[side, chunk], recv_sem=scale_recv.at[side, chunk],
                device_id={"ifg": there}, device_id_type=MESH,
            ))
        return copies

    def pack(value, side, chunk):
        top = jnp.max(jnp.abs(value), axis=0, keepdims=True)
        factor = 32766.0 / jnp.maximum(top, 1e-30)
        rounded = jnp.round(value * factor).astype(jnp.int32).astype(jnp.int16)
        sums_out[side, chunk] = rounded
        unit = top * (1.0 / 32766.0)
        for piece in range(CPX // 128):
            scale_out[side, chunk, piece : piece + 1, :] = unit[:, piece * 128 : piece * 128 + 128]

    def finish(chunk):
        for copy in sum_copies(chunk):
            copy.wait_recv()
        columns = pl.ds(pl.multiple_of(chunk * CPX, 128), CPX)
        total = out[:, columns]
        for side in range(2):
            unit = jnp.concatenate(
                [scale_in[side, chunk, piece : piece + 1, :] for piece in range(CPX // 128)], axis=1
            )
            total = total + sums_in[side, chunk, 0:M, :].astype(jnp.int32).astype(jnp.float32) * unit
        out[:, columns] = total

    def work(half):
        left_rows = (128, 512 if half == 0 else 384)
        right_rows = (640, 384) if half == 0 else (512, 512)

        def step(chunk, carry):
            wait_raw(chunk, raw_recv, 1024)
            if half == 0:
                ahead = chunk + LOOK
                @pl.when(ahead < NC)
                def _():
                    send_raw(ahead, 1)
            pack(apply(w_left[half, :, 0 : left_rows[1]], chunk, *left_rows), 0, chunk)
            pack(apply(w_right[half, :, 0 : right_rows[1]], chunk, *right_rows), 1, chunk)
            out[:, pl.ds(pl.multiple_of(chunk * CPX, 128), CPX)] = apply(w_own[half], chunk, 0, 128)[0:M]
            for copy in sum_copies(chunk):
                copy.start()

            @pl.when(chunk >= LAG)
            def _():
                finish(chunk - LAG)

            return carry

        return step

    lax.fori_loop(0, NC // 2, work(0), 0)
    lax.fori_loop(NC // 2, NC, work(1), 0)
    for chunk in range(NC - LAG, NC):
        finish(chunk)

    def drain(chunk, carry):
        wait_raw(chunk, raw_send, 976)
        for copy in sum_copies(chunk):
            copy.wait_send()
        return carry

    lax.fori_loop(0, NC, drain, 0)


def local(phases, date_pairs, pair_counts, group_ids):
    rows = phases.shape[0]
    source = phases.reshape(rows, phases.shape[2])
    dates = date_pairs.reshape(2, 4, 8, 32).transpose(0, 2, 1, 3).reshape(2, 1024)
    groups = lax.dynamic_index_in_dim(group_ids, lax.axis_index("grp"), 0, keepdims=False)
    run_groups = groups.reshape(2, 8)[:, 0]
    picked = run_groups[:, None] == jnp.arange(16, dtype=jnp.int32)[None, :]
    counts = jnp.sum(jnp.where(picked, pair_counts[None, :], 0), axis=1)
    levels = jnp.array([128, 256, 512, 1024], jnp.int32)
    hot = (levels[:, None] == counts[None, :]).astype(jnp.float32).reshape(8, 1)
    hot = jnp.broadcast_to(hot, (8, 128))
    vmem = pl.BlockSpec(memory_space=pltpu.VMEM)
    solved = pl.pallas_call(
        body,
        out_shape=jax.ShapeDtypeStruct((M, PIX), jnp.float32),
        in_specs=[pl.BlockSpec(memory_space=pl.ANY), vmem, vmem],
        out_specs=vmem,
        scratch_shapes=[
            pltpu.VMEM((1024, PIX), jnp.bfloat16),
            pltpu.VMEM((4, MP, 256), jnp.float32),
            pltpu.VMEM((256, 1024), jnp.bfloat16),
            pltpu.VMEM((2, 8, 128), jnp.float32),
            pltpu.VMEM((2, 2 * MP, 128), jnp.bfloat16),
            pltpu.VMEM((2, 2 * MP, 512), jnp.bfloat16),
            pltpu.VMEM((2, 2 * MP, 512), jnp.bfloat16),
            pltpu.VMEM((2, NC, MP, CPX), jnp.int16),
            pltpu.VMEM((2, NC, MP, CPX), jnp.int16),
            pltpu.VMEM((2, NC, 8, 128), jnp.float32),
            pltpu.VMEM((2, NC, 8, 128), jnp.float32),
            pltpu.SemaphoreType.DMA((NC,)),
            pltpu.SemaphoreType.DMA((NC,)),
            pltpu.SemaphoreType.DMA((2,)),
            pltpu.SemaphoreType.DMA((2,)),
            pltpu.SemaphoreType.DMA((2, NC)),
            pltpu.SemaphoreType.DMA((2, NC)),
            pltpu.SemaphoreType.DMA((2, NC)),
            pltpu.SemaphoreType.DMA((2, NC)),
        ],
        compiler_params=pltpu.CompilerParams(
            collective_id=0, has_side_effects=True, vmem_limit_bytes=60 * 1024 * 1024
        ),
    )(source, dates, hot)
    return solved[None, :, :]


def solution(mesh):
    in_specs = (P("ifg", "grp", None), P(), P(), P(None, "ifg"))
    out_specs = P("grp", None, "ifg")
    return jax.shard_map(local, mesh=mesh, in_specs=in_specs, out_specs=out_specs, check_vma=False)
```

```python
import jax
import jax.numpy as jnp
from jax import lax
from jax.experimental import pallas as pl
from jax.experimental.pallas import tpu as pltpu
from jax.sharding import PartitionSpec as P

M = 200
MP = 208
PIX = 4096
CPX = 512
NC = PIX // CPX
LOOK = NC
LAG = 1
EDGE = 88
SEAM = 113
GAP = 128 - SEAM
MESH = pl.DeviceIdType.MESH
SAME = ((0, 0, 0), (0, -1, 128), (0, 1, 256), (0, -2, 384), (0, 2, 768))
NEXT = ((-1, -3, 512), (1, 3, 896))
FAR = ((-2, -4, 640), (2, 4, 640))


def split3(value):
    high = value.astype(jnp.bfloat16)
    rest = value - high.astype(jnp.float32)
    middle = rest.astype(jnp.bfloat16)
    low = (rest - middle.astype(jnp.float32)).astype(jnp.bfloat16)
    return high, middle, low


def body(
    src, dates, hot, out,
    land, halves, inverse, design, near_hot, w_own, w_near, w_left, w_right,
    sums_out, sums_in, scale_out, scale_in,
    raw_send, raw_recv, hot_send, hot_recv, sum_send, sum_recv, scale_send, scale_recv,
):
    me = lax.axis_index("ifg")
    core = lax.rem(me, 2)
    z = lax.rem(lax.div(me, 2), 8)
    x = lax.div(me, 16)

    def device(x_at, z_at, core_at):
        return lax.rem(x_at, 4) * 16 + lax.rem(z_at + 16, 8) * 2 + lax.rem(core_at, 2)

    left, right = device(x, z - 1, core), device(x, z + 1, core)

    barrier = pltpu.get_barrier_semaphore()

    def greet(step, carry):
        peer = device(x + lax.div(step, 2), z, core + lax.rem(step, 2))
        for offset in (-2, -1, 1, 2):
            there = device(x + lax.div(step, 2), z + offset, core + lax.rem(step, 2))
            pl.semaphore_signal(barrier, inc=1, device_id={"ifg": there}, device_id_type=MESH)

        @pl.when(step > 0)
        def _():
            pl.semaphore_signal(barrier, inc=1, device_id={"ifg": peer}, device_id_type=MESH)

        return carry

    lax.fori_loop(0, 8, greet, 0)
    pl.semaphore_wait(barrier, 39)

    hot_copies = []
    for slot, offset in enumerate((1, -1, 2, -2)):
        copy = pltpu.make_async_remote_copy(
            src_ref=hot, dst_ref=near_hot.at[slot], send_sem=hot_send.at[slot], recv_sem=hot_recv.at[slot],
            device_id={"ifg": device(x, z + offset, core)}, device_id_type=MESH,
        )
        copy.start()
        hot_copies.append(copy)

    my_rows = x * 32 + core * 16

    def raw_parts(block, chunk, x_at, core_at):
        helper, owner, first = block
        there = device(x_at, z + helper, core_at)
        owner_index = device(x_at, z + owner, core_at)
        columns = pl.ds(pl.multiple_of(owner_index * PIX + chunk * CPX, 128), CPX)
        rows = pl.ds(pl.multiple_of(first + my_rows, 16), 16)
        landing = pl.ds(pl.multiple_of(chunk * CPX, 128), CPX)
        return src.at[:, columns], land.at[rows, landing], there

    def send_raw(chunk, half):
        away = (FAR[half],) + NEXT

        def remote(block, x_at, core_at):
            source, target, there = raw_parts(block, chunk, x_at, core_at)
            pltpu.make_async_remote_copy(
                src_ref=source, dst_ref=target, send_sem=raw_send.at[chunk], recv_sem=raw_recv.at[chunk],
                device_id={"ifg": there}, device_id_type=MESH,
            ).start()

        for block in away:
            remote(block, x, core)

        def peer(step, carry):
            for block in away + SAME:
                remote(block, x + lax.div(step, 2), core + lax.rem(step, 2))
            return carry

        lax.fori_loop(1, 8, peer, 0)
        for block in SAME:
            source, target, _ = raw_parts(block, chunk, x, core)
            pltpu.make_async_copy(source, target, raw_recv.at[chunk]).start()

    def wait_raw(chunk, sem, rows):
        view = land.at[pl.ds(0, rows), pl.ds(pl.multiple_of(chunk * CPX, 128), CPX)]
        pltpu.make_async_copy(view, view, sem.at[chunk]).wait()

    for chunk in range(LOOK):
        send_raw(chunk, chunk // (NC // 2))

    date_at = lax.broadcasted_iota(jnp.int32, (256, 1024), 0)
    placed = jnp.where(dates[...] < SEAM, dates[...], dates[...] + GAP)
    signs = (date_at == placed[1:2, :]).astype(jnp.float32) - (date_at == placed[0:1, :]).astype(jnp.float32)
    design[...] = signs.astype(jnp.bfloat16)
    place = lax.broadcasted_iota(jnp.int32, (1, 1024), 1)
    pair = ((place >> 5) & 3) * 256 + (place >> 7) * 32 + (place & 31)
    down = lax.broadcasted_iota(jnp.int32, (128, 128), 0)
    across = lax.broadcasted_iota(jnp.int32, (128, 128), 1)
    eye = (down == across).astype(jnp.float32)
    for level in range(4):
        kept = (signs * (pair < (128 << level)).astype(jnp.float32)).astype(jnp.bfloat16)
        gram = lax.dot_general(
            design[...], kept, (((1,), (1,)), ((), ())), preferred_element_type=jnp.float32
        )
        halves[level] = gram[0:128, 0:128] + eye
        halves[4 + level] = (
            gram[128:256, 128:256] + gram[0:128, 128:256] + gram[128:256, 0:128] + jnp.where(down < EDGE, eye, 0.0)
        )

    def eliminate(work, rows, side, lanes):
        mine = slice(side * 128, side * 128 + 128)
        rest = [slice(at * 128, at * 128 + 128) for at in range(lanes // 128) if at != side]
        lane = lax.broadcasted_iota(jnp.int32, (1, 1, lanes), 2)
        lane_mine = lax.broadcasted_iota(jnp.int32, (1, 1, 128), 2)

        def step(index, carry):
            hit = lane_mine == index - side * 128
            row = work[:, pl.ds(index, 1), :]
            block = work[:, 0:rows, mine]
            column = jnp.sum(jnp.where(hit, block, 0.0), axis=2, keepdims=True)
            pivot = 1.0 / jnp.sum(jnp.where(hit, row[:, :, mine], 0.0), axis=2, keepdims=True)
            scaled = jnp.where(lane == index, pivot, row * pivot)
            work[:, 0:rows, mine] = jnp.where(hit, 0.0, block) - column * scaled[:, :, mine]
            for other in rest:
                work[:, 0:rows, other] = work[:, 0:rows, other] - column * scaled[:, :, other]
            work[:, pl.ds(index, 1), :] = scaled
            return carry

        return step

    lax.fori_loop(0, EDGE, eliminate(halves, 120, 0, 128), 0)
    low_row, low_lane = down < EDGE, across < EDGE
    for level in range(4):
        after = halves[4 + level]
        inverse[level, 0:128, 0:128] = halves[level] + jnp.where(low_row | low_lane, 0.0, after)
        inverse[level, 0:128, 128:256] = jnp.where(low_lane & ~low_row, after, 0.0)
        inverse[level, 128:216, 0:128] = jnp.where(low_row & ~low_lane, after, 0.0)[0:EDGE]
        inverse[level, 128:216, 128:256] = jnp.where(low_row & low_lane, after, 0.0)[0:EDGE]
    lax.fori_loop(EDGE, SEAM, eliminate(inverse, 216, 0, 256), 0)

    for copy in hot_copies:
        copy.wait()

    def weights(flags, run, blocks, target):
        flag = [flags[2 * level + run : 2 * level + run + 1, 0:1] for level in range(4)]
        chosen = sum(flag[level] * inverse[level] for level in range(4))
        chosen = jnp.concatenate([chosen[0:SEAM], chosen[128 : 128 + M - SEAM], jnp.zeros((MP - M, 256), jnp.float32)])
        parts = split3(chosen)
        column = lax.broadcasted_iota(jnp.int32, (1, 128), 1)
        for at, offset in enumerate(blocks):
            z_at = lax.rem(z + offset + 16, 8)
            block = design[:, pl.ds(pl.multiple_of(z_at * 128, 128), 128)]
            value = sum(jnp.dot(part, block, preferred_element_type=jnp.float32) for part in parts)
            pair_at = (column >> 5) * 256 + z_at * 32 + (column & 31)
            value = value * sum(flag[level] * (pair_at < (128 << level)).astype(jnp.float32) for level in range(4))
            high = value.astype(jnp.bfloat16)
            low = (value - high.astype(jnp.float32)).astype(jnp.bfloat16)
            target[0:MP, at * 128 : at * 128 + 128] = high
            target[MP : 2 * MP, at * 128 : at * 128 + 128] = low

    for run in range(2):
        weights(near_hot.at[2], run, (0, 1, 2)[: 3 - run], w_left.at[run])
        weights(near_hot.at[3], run, (0, -1) if run == 0 else (-2, 0, -1), w_right.at[run])
        weights(near_hot.at[0], run, (0,), w_near.at[0, run])
        weights(near_hot.at[1], run, (0,), w_near.at[1, run])
        weights(hot, run, (0,), w_own.at[run])

    def apply(weight, chunk, first, depth):
        data = land[first : first + depth, pl.ds(pl.multiple_of(chunk * CPX, 128), CPX)]
        both = jnp.dot(weight, data, preferred_element_type=jnp.float32)
        return both[0:MP] + both[MP : 2 * MP]

    def sum_copies(stage, chunk):
        copies = []
        for side, there in ((0, left), (1, right)):
            copies.append(pltpu.make_async_remote_copy(
                src_ref=sums_out.at[stage, side, chunk], dst_ref=sums_in.at[stage, side, chunk],
                send_sem=sum_send.at[stage, side, chunk], recv_sem=sum_recv.at[stage, side, chunk],
                device_id={"ifg": there}, device_id_type=MESH,
            ))
            copies.append(pltpu.make_async_remote_copy(
                src_ref=scale_out.at[stage, side, chunk], dst_ref=scale_in.at[stage, side, chunk],
                send_sem=scale_send.at[stage, side, chunk], recv_sem=scale_recv.at[stage, side, chunk],
                device_id={"ifg": there}, device_id_type=MESH,
            ))
        return copies

    def pack(value, stage, side, chunk):
        top = jnp.max(jnp.abs(value), axis=0, keepdims=True)
        factor = 32766.0 / jnp.maximum(top, 1e-30)
        rounded = jnp.round(value * factor).astype(jnp.int32).astype(jnp.int16)
        sums_out[stage, side, chunk] = rounded
        unit = top * (1.0 / 32766.0)
        for piece in range(CPX // 128):
            scale_out[stage, side, chunk, piece : piece + 1, :] = unit[:, piece * 128 : piece * 128 + 128]

    def unpack(stage, side, chunk, rows):
        unit = jnp.concatenate(
            [scale_in[stage, side, chunk, piece : piece + 1, :] for piece in range(CPX // 128)], axis=1
        )
        return sums_in[stage, side, chunk, 0:rows, :].astype(jnp.int32).astype(jnp.float32) * unit

    def relay(chunk, run):
        for copy in sum_copies(0, chunk):
            copy.wait_recv()
        for side in range(2):
            pack(apply(w_near[side, run], chunk, 128 + 128 * side, 128) + unpack(0, side, chunk, MP), 1, side, chunk)
        for copy in sum_copies(1, chunk):
            copy.start()

    def finish(chunk, run):
        columns = pl.ds(pl.multiple_of(chunk * CPX, 128), CPX)
        own = apply(w_own[run], chunk, 0, 128)[0:M]
        for copy in sum_copies(1, chunk):
            copy.wait_recv()
        out[:, columns] = own + unpack(1, 0, chunk, M) + unpack(1, 1, chunk, M)

    half_count = NC // 2

    def work(half):
        left_depth, right_first = (384, 768) if half == 0 else (256, 640)

        def step(chunk, carry):
            wait_raw(chunk, raw_recv, 1024)
            if half == 0:
                ahead = chunk + LOOK

                @pl.when(ahead < NC)
                def _():
                    send_raw(ahead, 1)

            pack(apply(w_left[half, :, 0:left_depth], chunk, 384, left_depth), 0, 0, chunk)
            pack(apply(w_right[half, :, 0 : 1024 - right_first], chunk, right_first, 1024 - right_first), 0, 1, chunk)
            for copy in sum_copies(0, chunk):
                copy.start()

            @pl.when(chunk >= LAG)
            def _():
                relay(chunk - LAG, lax.div(chunk - LAG, half_count))

            @pl.when(chunk >= 2 * LAG)
            def _():
                finish(chunk - 2 * LAG, lax.div(chunk - 2 * LAG, half_count))

            return carry

        return step

    lax.fori_loop(0, half_count, work(0), 0)
    lax.fori_loop(half_count, NC, work(1), 0)
    for chunk in range(NC - LAG, NC):
        relay(chunk, 1)
    for chunk in range(NC - 2 * LAG, NC):
        finish(chunk, 1)

    def drain(chunk, carry):
        wait_raw(chunk, raw_send, 944)
        for copy in sum_copies(0, chunk) + sum_copies(1, chunk):
            copy.wait_send()
        return carry

    lax.fori_loop(0, NC, drain, 0)


def local(phases, date_pairs, pair_counts, group_ids):
    rows = phases.shape[0]
    source = phases.reshape(rows, phases.shape[2])
    dates = date_pairs.reshape(2, 4, 8, 32).transpose(0, 2, 1, 3).reshape(2, 1024)
    groups = lax.dynamic_index_in_dim(group_ids, lax.axis_index("grp"), 0, keepdims=False)
    run_groups = groups.reshape(2, 8)[:, 0]
    picked = run_groups[:, None] == jnp.arange(16, dtype=jnp.int32)[None, :]
    counts = jnp.sum(jnp.where(picked, pair_counts[None, :], 0), axis=1)
    levels = jnp.array([128, 256, 512, 1024], jnp.int32)
    hot = (levels[:, None] == counts[None, :]).astype(jnp.float32).reshape(8, 1)
    hot = jnp.broadcast_to(hot, (8, 128))
    vmem = pl.BlockSpec(memory_space=pltpu.VMEM)
    solved = pl.pallas_call(
        body,
        out_shape=jax.ShapeDtypeStruct((M, PIX), jnp.float32),
        in_specs=[pl.BlockSpec(memory_space=pl.ANY), vmem, vmem],
        out_specs=vmem,
        scratch_shapes=[
            pltpu.VMEM((1024, PIX), jnp.bfloat16),
            pltpu.VMEM((8, 128, 128), jnp.float32),
            pltpu.VMEM((4, 216, 256), jnp.float32),
            pltpu.VMEM((256, 1024), jnp.bfloat16),
            pltpu.VMEM((4, 8, 128), jnp.float32),
            pltpu.VMEM((2, 2 * MP, 128), jnp.bfloat16),
            pltpu.VMEM((2, 2, 2 * MP, 128), jnp.bfloat16),
            pltpu.VMEM((2, 2 * MP, 384), jnp.bfloat16),
            pltpu.VMEM((2, 2 * MP, 384), jnp.bfloat16),
            pltpu.VMEM((2, 2, NC, MP, CPX), jnp.int16),
            pltpu.VMEM((2, 2, NC, MP, CPX), jnp.int16),
            pltpu.VMEM((2, 2, NC, 8, 128), jnp.float32),
            pltpu.VMEM((2, 2, NC, 8, 128), jnp.float32),
            pltpu.SemaphoreType.DMA((NC,)),
            pltpu.SemaphoreType.DMA((NC,)),
            pltpu.SemaphoreType.DMA((4,)),
            pltpu.SemaphoreType.DMA((4,)),
            pltpu.SemaphoreType.DMA((2, 2, NC)),
            pltpu.SemaphoreType.DMA((2, 2, NC)),
            pltpu.SemaphoreType.DMA((2, 2, NC)),
            pltpu.SemaphoreType.DMA((2, 2, NC)),
        ],
        compiler_params=pltpu.CompilerParams(
            collective_id=0, has_side_effects=True, vmem_limit_bytes=60 * 1024 * 1024
        ),
    )(source, dates, hot)
    return solved[None, :, :]


def solution(mesh):
    in_specs = (P("ifg", "grp", None), P(), P(), P(None, "ifg"))
    out_specs = P("grp", None, "ifg")
    return jax.shard_map(local, mesh=mesh, in_specs=in_specs, out_specs=out_specs, check_vma=False)
```

```python
import jax
import jax.numpy as jnp
from jax import lax
from jax.experimental import pallas as pl
from jax.experimental.pallas import tpu as pltpu
from jax.sharding import PartitionSpec as P

M = 200
MP = 208
PIX = 4096
CPX = 512
NC = PIX // CPX
LEAD = 1
LAG = 1
EDGE = 88
SEAM = 113
GAP = 128 - SEAM
MESH = pl.DeviceIdType.MESH
SAME = ((0, 0, 0), (0, -1, 128), (0, 1, 256), (0, -2, 384), (0, 2, 768))
NEXT = ((-1, -3, 512), (1, 3, 896))
FAR = ((-2, -4, 640), (2, 4, 640))


def split3(value):
    high = value.astype(jnp.bfloat16)
    rest = value - high.astype(jnp.float32)
    middle = rest.astype(jnp.bfloat16)
    low = (rest - middle.astype(jnp.float32)).astype(jnp.bfloat16)
    return high, middle, low


def body(
    src, date_pairs, pair_counts, group_ids, out,
    land, halves, inverse, design, near_hot, w_own, w_near, w_left, w_right,
    sums_out, sums_in, scale_out, scale_in, total, hot,
    raw_send, raw_recv, hot_send, hot_recv, sum_send, sum_recv, scale_send, scale_recv, out_sem,
):
    me = lax.axis_index("ifg")
    core = lax.rem(me, 2)
    z = lax.rem(lax.div(me, 2), 8)
    x = lax.div(me, 16)

    def device(x_at, z_at, core_at):
        return lax.rem(x_at, 4) * 16 + lax.rem(z_at + 16, 8) * 2 + lax.rem(core_at, 2)

    left, right = device(x, z - 1, core), device(x, z + 1, core)

    barrier = pltpu.get_barrier_semaphore()

    def greet(step, carry):
        peer = device(x + lax.div(step, 2), z, core + lax.rem(step, 2))
        for offset in (-2, -1, 1, 2):
            there = device(x + lax.div(step, 2), z + offset, core + lax.rem(step, 2))
            pl.semaphore_signal(barrier, inc=1, device_id={"ifg": there}, device_id_type=MESH)

        @pl.when(step > 0)
        def _():
            pl.semaphore_signal(barrier, inc=1, device_id={"ifg": peer}, device_id_type=MESH)

        return carry

    lax.fori_loop(0, 8, greet, 0)
    pl.semaphore_wait(barrier, 39)

    my_rows = x * 32 + core * 16

    def raw_parts(block, chunk, x_at, core_at):
        helper, owner, first = block
        there = device(x_at, z + helper, core_at)
        owner_index = device(x_at, z + owner, core_at)
        columns = pl.ds(pl.multiple_of(owner_index * PIX + chunk * CPX, 128), CPX)
        rows = pl.ds(pl.multiple_of(first + my_rows, 16), 16)
        landing = pl.ds(pl.multiple_of(chunk * CPX, 128), CPX)
        return src.at[:, columns], land.at[rows, landing], there

    def send_one(block, chunk, x_at, core_at):
        source, target, there = raw_parts(block, chunk, x_at, core_at)
        pltpu.make_async_remote_copy(
            src_ref=source, dst_ref=target, send_sem=raw_send.at[chunk], recv_sem=raw_recv.at[chunk],
            device_id={"ifg": there}, device_id_type=MESH,
        ).start()

    def send_away(chunk, half):
        def peer(step, carry):
            for block in (FAR[half],) + NEXT:
                send_one(block, chunk, x + lax.div(step, 2), core + lax.rem(step, 2))
            return carry

        lax.fori_loop(0, 8, peer, 0)

    def send_same(chunk):
        def peer(step, carry):
            for block in SAME:
                send_one(block, chunk, x + lax.div(step, 2), core + lax.rem(step, 2))
            return carry

        lax.fori_loop(1, 8, peer, 0)
        for block in SAME:
            source, target, _ = raw_parts(block, chunk, x, core)
            pltpu.make_async_copy(source, target, raw_recv.at[chunk]).start()

    def wait_raw(chunk, sem, rows):
        view = land.at[pl.ds(0, rows), pl.ds(pl.multiple_of(chunk * CPX, 128), CPX)]
        pltpu.make_async_copy(view, view, sem.at[chunk]).wait()

    for chunk in range(NC + LEAD):
        if chunk < NC:
            send_away(chunk, chunk // (NC // 2))
        if chunk >= LEAD:
            send_same(chunk - LEAD)

    groups = group_ids[pl.ds(lax.axis_index("grp"), 1), :]
    counts = sum(jnp.where(groups == group, pair_counts[group], 0) for group in range(16))
    for level in range(4):
        for run in range(2):
            flag = (counts[:, 8 * run : 8 * run + 1] == (128 << level)).astype(jnp.float32)
            hot[2 * level + run : 2 * level + run + 1, :] = jnp.broadcast_to(flag, (1, 128))
    hot_copies = []
    for slot, offset in enumerate((1, -1, 2, -2)):
        copy = pltpu.make_async_remote_copy(
            src_ref=hot, dst_ref=near_hot.at[slot], send_sem=hot_send.at[slot], recv_sem=hot_recv.at[slot],
            device_id={"ifg": device(x, z + offset, core)}, device_id_type=MESH,
        )
        copy.start()
        hot_copies.append(copy)

    date_at = lax.broadcasted_iota(jnp.int32, (256, 1024), 0)
    dates = jnp.concatenate(
        [date_pairs[:, at * 256 + row * 32 : at * 256 + row * 32 + 32] for row in range(8) for at in range(4)], axis=1
    )
    placed = jnp.where(dates < SEAM, dates, dates + GAP)
    signs = (date_at == placed[1:2, :]).astype(jnp.float32) - (date_at == placed[0:1, :]).astype(jnp.float32)
    design[...] = signs.astype(jnp.bfloat16)
    place = lax.broadcasted_iota(jnp.int32, (1, 1024), 1)
    pair = ((place >> 5) & 3) * 256 + (place >> 7) * 32 + (place & 31)
    down = lax.broadcasted_iota(jnp.int32, (128, 128), 0)
    across = lax.broadcasted_iota(jnp.int32, (128, 128), 1)
    eye = (down == across).astype(jnp.float32)
    for level in range(4):
        kept = (signs * (pair < (128 << level)).astype(jnp.float32)).astype(jnp.bfloat16)
        gram = lax.dot_general(
            design[...], kept, (((1,), (1,)), ((), ())), preferred_element_type=jnp.float32
        )
        halves[level] = gram[0:128, 0:128] + eye
        halves[4 + level] = (
            gram[128:256, 128:256] + gram[0:128, 128:256] + gram[128:256, 0:128] + jnp.where(down < EDGE, eye, 0.0)
        )

    def eliminate(work, rows, side, lanes):
        mine = slice(side * 128, side * 128 + 128)
        rest = [slice(at * 128, at * 128 + 128) for at in range(lanes // 128) if at != side]
        lane = lax.broadcasted_iota(jnp.int32, (1, 1, lanes), 2)
        lane_mine = lax.broadcasted_iota(jnp.int32, (1, 1, 128), 2)

        def step(index, carry):
            hit = lane_mine == index - side * 128
            row = work[:, pl.ds(index, 1), :]
            block = work[:, 0:rows, mine]
            column = jnp.sum(jnp.where(hit, block, 0.0), axis=2, keepdims=True)
            pivot = 1.0 / jnp.sum(jnp.where(hit, row[:, :, mine], 0.0), axis=2, keepdims=True)
            scaled = jnp.where(lane == index, pivot, row * pivot)
            work[:, 0:rows, mine] = jnp.where(hit, 0.0, block) - column * scaled[:, :, mine]
            for other in rest:
                work[:, 0:rows, other] = work[:, 0:rows, other] - column * scaled[:, :, other]
            work[:, pl.ds(index, 1), :] = scaled
            return carry

        return step

    lax.fori_loop(0, EDGE, eliminate(halves, 120, 0, 128), 0)
    low_row, low_lane = down < EDGE, across < EDGE
    for level in range(4):
        after = halves[4 + level]
        inverse[level, 0:128, 0:128] = halves[level] + jnp.where(low_row | low_lane, 0.0, after)
        inverse[level, 0:128, 128:256] = jnp.where(low_lane & ~low_row, after, 0.0)
        inverse[level, 128:216, 0:128] = jnp.where(low_row & ~low_lane, after, 0.0)[0:EDGE]
        inverse[level, 128:216, 128:256] = jnp.where(low_row & low_lane, after, 0.0)[0:EDGE]
    lax.fori_loop(EDGE, SEAM, eliminate(inverse, 216, 0, 256), 0)

    for copy in hot_copies:
        copy.wait()

    def weights(flags, run, blocks, target):
        flag = [flags[2 * level + run : 2 * level + run + 1, 0:1] for level in range(4)]
        chosen = sum(flag[level] * inverse[level] for level in range(4))
        chosen = jnp.concatenate([chosen[0:SEAM], chosen[128 : 128 + M - SEAM], jnp.zeros((MP - M, 256), jnp.float32)])
        parts = split3(chosen)
        column = lax.broadcasted_iota(jnp.int32, (1, 128), 1)
        for at, offset in enumerate(blocks):
            z_at = lax.rem(z + offset + 16, 8)
            block = design[:, pl.ds(pl.multiple_of(z_at * 128, 128), 128)]
            value = sum(jnp.dot(part, block, preferred_element_type=jnp.float32) for part in parts)
            pair_at = (column >> 5) * 256 + z_at * 32 + (column & 31)
            value = value * sum(flag[level] * (pair_at < (128 << level)).astype(jnp.float32) for level in range(4))
            high = value.astype(jnp.bfloat16)
            low = (value - high.astype(jnp.float32)).astype(jnp.bfloat16)
            target[0:MP, at * 128 : at * 128 + 128] = high
            target[MP : 2 * MP, at * 128 : at * 128 + 128] = low

    for run in range(2):
        weights(near_hot.at[2], run, (0, 1, 2)[: 3 - run], w_left.at[run])
        weights(near_hot.at[3], run, (0, -1) if run == 0 else (-2, 0, -1), w_right.at[run])
        weights(near_hot.at[0], run, (0,), w_near.at[0, run])
        weights(near_hot.at[1], run, (0,), w_near.at[1, run])
        weights(hot, run, (0,), w_own.at[run])

    def apply(weight, chunk, first, depth):
        data = land[first : first + depth, pl.ds(pl.multiple_of(chunk * CPX, 128), CPX)]
        both = jnp.dot(weight, data, preferred_element_type=jnp.float32)
        return both[0:M] + both[MP : MP + M]

    def sum_copies(stage, chunk):
        copies = []
        for side, there in ((0, left), (1, right)):
            copies.append(pltpu.make_async_remote_copy(
                src_ref=sums_out.at[stage, side, chunk], dst_ref=sums_in.at[stage, side, chunk],
                send_sem=sum_send.at[stage, side, chunk], recv_sem=sum_recv.at[stage, side, chunk],
                device_id={"ifg": there}, device_id_type=MESH,
            ))
            copies.append(pltpu.make_async_remote_copy(
                src_ref=scale_out.at[stage, side, chunk], dst_ref=scale_in.at[stage, side, chunk],
                send_sem=scale_send.at[stage, side, chunk], recv_sem=scale_recv.at[stage, side, chunk],
                device_id={"ifg": there}, device_id_type=MESH,
            ))
        return copies

    def pack(value, stage, side, chunk):
        top = jnp.max(jnp.abs(value), axis=0, keepdims=True)
        factor = 32766.0 / jnp.maximum(top, 1e-30)
        rounded = jnp.round(value * factor).astype(jnp.int32).astype(jnp.int16)
        sums_out[stage, side, chunk] = rounded
        unit = top * (1.0 / 32766.0)
        for piece in range(CPX // 128):
            scale_out[stage, side, chunk, piece : piece + 1, :] = unit[:, piece * 128 : piece * 128 + 128]

    def unpack(stage, side, chunk):
        unit = jnp.concatenate(
            [scale_in[stage, side, chunk, piece : piece + 1, :] for piece in range(CPX // 128)], axis=1
        )
        return sums_in[stage, side, chunk].astype(jnp.int32).astype(jnp.float32) * unit

    def result_copy(chunk):
        columns = pl.ds(pl.multiple_of(chunk * CPX, 128), CPX)
        return pltpu.make_async_copy(total.at[chunk], out.at[:, columns], out_sem.at[chunk])

    def relay(chunk, run):
        for copy in sum_copies(0, chunk):
            copy.wait_recv()
        for side in range(2):
            pack(apply(w_near[side, run], chunk, 128 + 128 * side, 128) + unpack(0, side, chunk), 1, side, chunk)
        for copy in sum_copies(1, chunk):
            copy.start()

    def finish(chunk, run):
        own = apply(w_own[run], chunk, 0, 128)
        for copy in sum_copies(1, chunk):
            copy.wait_recv()
        total[chunk] = own + unpack(1, 0, chunk) + unpack(1, 1, chunk)
        result_copy(chunk).start()

    half_count = NC // 2

    def work(half):
        left_depth, right_first = (384, 768) if half == 0 else (256, 640)

        def step(chunk, carry):
            wait_raw(chunk, raw_recv, 1024)
            pack(apply(w_left[half, :, 0:left_depth], chunk, 384, left_depth), 0, 0, chunk)
            pack(apply(w_right[half, :, 0 : 1024 - right_first], chunk, right_first, 1024 - right_first), 0, 1, chunk)
            for copy in sum_copies(0, chunk):
                copy.start()

            @pl.when(chunk >= LAG)
            def _():
                relay(chunk - LAG, lax.div(chunk - LAG, half_count))

            @pl.when(chunk >= 2 * LAG)
            def _():
                finish(chunk - 2 * LAG, lax.div(chunk - 2 * LAG, half_count))

            return carry

        return step

    lax.fori_loop(0, half_count, work(0), 0)
    lax.fori_loop(half_count, NC, work(1), 0)
    for chunk in range(NC - LAG, NC):
        relay(chunk, 1)
    for chunk in range(NC - 2 * LAG, NC):
        finish(chunk, 1)

    def drain(chunk, carry):
        wait_raw(chunk, raw_send, 944)
        for copy in sum_copies(0, chunk) + sum_copies(1, chunk):
            copy.wait_send()
        result_copy(chunk).wait()
        return carry

    lax.fori_loop(0, NC, drain, 0)


def local(phases, date_pairs, pair_counts, group_ids):
    rows = phases.shape[0]
    source = phases.reshape(rows, phases.shape[2])
    vmem = pl.BlockSpec(memory_space=pltpu.VMEM)
    solved = pl.pallas_call(
        body,
        out_shape=jax.ShapeDtypeStruct((M, PIX), jnp.float32),
        in_specs=[pl.BlockSpec(memory_space=pl.ANY), vmem, pl.BlockSpec(memory_space=pltpu.SMEM), vmem],
        out_specs=pl.BlockSpec(memory_space=pl.ANY),
        scratch_shapes=[
            pltpu.VMEM((1024, PIX), jnp.bfloat16),
            pltpu.VMEM((8, 128, 128), jnp.float32),
            pltpu.VMEM((4, 216, 256), jnp.float32),
            pltpu.VMEM((256, 1024), jnp.bfloat16),
            pltpu.VMEM((4, 8, 128), jnp.float32),
            pltpu.VMEM((2, 2 * MP, 128), jnp.bfloat16),
            pltpu.VMEM((2, 2, 2 * MP, 128), jnp.bfloat16),
            pltpu.VMEM((2, 2 * MP, 384), jnp.bfloat16),
            pltpu.VMEM((2, 2 * MP, 384), jnp.bfloat16),
            pltpu.VMEM((2, 2, NC, M, CPX), jnp.int16),
            pltpu.VMEM((2, 2, NC, M, CPX), jnp.int16),
            pltpu.VMEM((2, 2, NC, CPX // 128, 128), jnp.float32),
            pltpu.VMEM((2, 2, NC, CPX // 128, 128), jnp.float32),
            pltpu.VMEM((NC, M, CPX), jnp.float32),
            pltpu.VMEM((8, 128), jnp.float32),
            pltpu.SemaphoreType.DMA((NC,)),
            pltpu.SemaphoreType.DMA((NC,)),
            pltpu.SemaphoreType.DMA((4,)),
            pltpu.SemaphoreType.DMA((4,)),
            pltpu.SemaphoreType.DMA((2, 2, NC)),
            pltpu.SemaphoreType.DMA((2, 2, NC)),
            pltpu.SemaphoreType.DMA((2, 2, NC)),
            pltpu.SemaphoreType.DMA((2, 2, NC)),
            pltpu.SemaphoreType.DMA((NC,)),
        ],
        compiler_params=pltpu.CompilerParams(
            collective_id=0, has_side_effects=True, vmem_limit_bytes=48 * 1024 * 1024
        ),
    )(source, date_pairs, pair_counts, group_ids)
    return solved[None, :, :]


def solution(mesh):
    in_specs = (P("ifg", "grp", None), P(), P(), P(None, "ifg"))
    out_specs = P("grp", None, "ifg")
    return jax.shard_map(local, mesh=mesh, in_specs=in_specs, out_specs=out_specs, check_vma=False)
```
